128 devices in a mesh: outer: 8 (over z, core), inner: 16 (over x, y).
Axes of the slice: x: 4, y: 4, z: 4, core: 2. Of those that a mesh axis runs over, the one named last changes fastest.
Arguments:
- patches: bfloat16 [512, 128, 1024], P(('outer', 'inner')), may hold values from -6 to 6
- cotangent: bfloat16 [512, 128, 1024], P(('outer', 'inner')), may hold values from -0.140625 to 0.140625
- segment_ids: int32 [512, 128], P(('outer', 'inner')), may hold values from 0 to 7, never falling along the last dimension, each value on 1 to 64 neighbouring positions
- live_packs: int32 [128], P(('outer', 'inner')), may hold values from 1 to 4, as said below
- norm_gain: float32 [1024], replicated, may hold values from 0.25 to 1.75
- qkv_weight: bfloat16 [1024, 3072], P('inner'), may hold values from -0.1875 to 0.1875
- out_weight: bfloat16 [1024, 1024], P('inner'), may hold values from -0.1875 to 0.1875
- signs_qkv: int32 [3072], replicated, may hold values from 0 to 1
- signs_out: int32 [1024], replicated, may hold values from 0 to 1
Outputs:
- qkv_grad: float32 [1024, 3072], P('inner')
- out_grad: float32 [1024, 1024], P('inner')
- gain_grad: float32 [1024], replicated
The draws below stay inside these ranges and needn't reach their ends.
Inputs may be any that keep to these rules, and one draw needn't show every extreme that they name: `live_packs`: the live slots of a device are its first ones; in every draw some device has all 4 slots live.
All inputs are finite; a program needn't handle non-finite values.
Results may differ from the reference program's by a relative error of at most 0.03.
Values may be sent and summed in bfloat16 or wider, within the bound.
No kernel may reach another device: no remote copies, remote signals or barrier semaphores. Data moves between devices by JAX's collectives and lax.ppermute only.
A program may use at most 64 MiB of HBM per device.

```python
import math
import jax
import jax.numpy as jnp
import numpy as np
from jax import lax

D = 1024
HEAD_DIM = 64
L = 128
PACKS_DEV = 4
PACKS = 512
N_OUTER = 8
N_INNER = 16


def draw_live_packs(key, part):
    device_count = N_OUTER * N_INNER
    picked = jax.random.randint(key, (device_count,), 1, PACKS_DEV + 1)
    loads = jnp.maximum(1, picked * picked // PACKS_DEV)
    busiest = jax.random.randint(jax.random.fold_in(key, 7), (), 0, device_count)
    loads = jnp.where(jnp.arange(device_count) == busiest, PACKS_DEV, loads)
    return loads.astype(jnp.int32)


def draw_qkv_weight(key, part):
    main_key = jax.random.fold_in(key, 11)
    whole = jax.random.truncated_normal(main_key, -5.0, 5.0, (D, 3 * D), jnp.float32) * D ** (-0.5)
    return whole.astype(jnp.bfloat16)


def draw_patches(key, part):
    main_key = jax.random.fold_in(key, 21)
    whole = jax.random.truncated_normal(main_key, -6.0, 6.0, (PACKS, L, D), jnp.float32)
    return whole.astype(jnp.bfloat16)


def with_ends(result, own_key, smallest, largest):
    place = [jax.random.randint(jax.random.fold_in(own_key, axis), (), 0, length) for axis, length in enumerate(result.shape)]
    widest = result.shape.index(max(result.shape))
    neighbour = place[:widest] + [(place[widest] + 1) % result.shape[widest]] + place[widest + 1:]
    return result.at[tuple(place)].set(smallest).at[tuple(neighbour)].set(largest)


def shard_levels(stream_key, dims, cuts, least, high):
    level = 1.0
    for axis_at, blocks in cuts:
        heights = jax.random.uniform(jax.random.fold_in(jax.random.fold_in(stream_key, 6), axis_at), (blocks,), jnp.float32, least / len(cuts), high / len(cuts))
        level = level * jnp.repeat(jnp.exp(heights), dims[axis_at] // blocks).reshape((-1,) + (1,) * (len(dims) - 1 - axis_at))
    return level


def profile(number_of, total, bound, skew):
    portions = [(1 << 20) // math.isqrt(rank ** skew) + 1 for rank in range(2, number_of + 1)]
    spare, holding = total - bound - (number_of - 1), [1] * (number_of - 1)
    while spare > 0:
        movable = [i for i in range(number_of - 1) if holding[i] < bound]
        mass, budget = sum([portions[i] for i in movable]), spare
        for i in movable:
            more = min(bound - holding[i], max(1, budget * portions[i] // mass), spare)
            holding[i] = holding[i] + more
            spare = spare - more
    return np.array([bound] + holding)


def ragged_sizes(key, amount, total, bound, slope):
    if amount == 2:
        one = jax.random.randint(key, (), max(1, total - bound), min(bound, total - 1) + 1)
        return jnp.stack([one, total - one])
    sizes = jnp.asarray(profile(amount, total, bound, slope), jnp.int32)
    couples = (amount - 1) // 2
    source_of, receiver = sizes[1:1 + 2 * couples:2], sizes[2:2 + 2 * couples:2]
    room = jnp.minimum(source_of - 1, bound - receiver)
    passed = jax.random.randint(jax.random.fold_in(key, 1), (couples,), 0, 1 << 20) % (room + 1)
    sizes = sizes.at[1:1 + 2 * couples:2].set(source_of - passed).at[2:2 + 2 * couples:2].set(receiver + passed)
    return sizes[jax.random.permutation(jax.random.fold_in(key, 2), amount)]


def gaussian(key, dims, width, bound, pieces=(), held_as=jnp.bfloat16):
    drawn = jax.random.normal(key, dims, jnp.float32) * width
    if len(pieces) > 0:
        drawn = shard_levels(key, dims, pieces, -0.22, 0.18) * drawn
    return jnp.clip(drawn, min=-bound, max=bound).astype(held_as)


def setup_inputs(seed: int = 0) -> dict:
    seeds = jax.random.split(jax.random.key(seed), 10)
    return {
        "patches": draw_patches(jax.random.fold_in(seeds[9], 71), 0),
        "cotangent": gaussian(seeds[1], (PACKS, L, D), (6 * (PACKS_DEV * L * N_OUTER * N_INNER) ** -0.5), 0.140625, ((0, 128),)),
        "segment_ids": jax.vmap(lambda own: jnp.searchsorted(jnp.cumsum(ragged_sizes(own, 8, L, L // 2, 0)), jnp.arange(L), side="right"))(jax.random.split(seeds[2], PACKS)).reshape((PACKS, L)).astype(jnp.int32),
        "live_packs": draw_live_packs(jax.random.fold_in(seeds[9], 71), 0),
        "norm_gain": jnp.clip(1.0 + 0.15 * jax.random.normal(seeds[4], (D,), jnp.float32), 0.25, 1.75),
        "qkv_weight": draw_qkv_weight(jax.random.fold_in(seeds[9], 71), 0),
        "out_weight": gaussian(seeds[6], (D, D), D ** -0.5, 0.1875, ((0, 16),)),
        "signs_qkv": with_ends(jax.random.randint(seeds[7], (3 * D,), 0, 2), jax.random.fold_in(seeds[7], 1), 0, 1).astype(jnp.int32),
        "signs_out": with_ends(jax.random.randint(seeds[8], (D,), 0, 2), jax.random.fold_in(seeds[8], 1), 0, 1).astype(jnp.int32),
    }


EPSILON = 1e-06
CLIP_RATIO = 2.0
BLOCK_WIDTH = 128
BLOCK_SCALE = 0.08838834764831845

def hadamard_table():
    indices = jnp.arange(BLOCK_WIDTH, dtype=jnp.int32)
    common = jnp.zeros((BLOCK_WIDTH, BLOCK_WIDTH), jnp.int32)
    for level in range(7):
        stride = 2 ** level
        common = common + indices[:, None] // stride % 2 * (indices[None, :] // stride % 2)
    return (1 - 2 * (common % 2)).astype(jnp.float32) * BLOCK_SCALE

def normalize(inputs, norm_gain):
    center = inputs - lax.optimization_barrier(jnp.mean(inputs, axis=-1, keepdims=True))
    spread = lax.optimization_barrier(jnp.mean(center * center, axis=-1, keepdims=True))
    return center * lax.rsqrt(spread + EPSILON) * norm_gain

def attend(projected, segment_ids):
    pack_count, pack_length, triple_width = projected.shape
    model_width = triple_width // 3
    head_count = model_width // HEAD_DIM
    split = projected.astype(jnp.float32).reshape(pack_count, pack_length, 3, head_count, HEAD_DIM)
    queries = split[:, :, 0]
    keys_all = split[:, :, 1]
    values_all = split[:, :, 2]
    scores = jnp.einsum('bqhd,bkhd->bhqk', queries, keys_all) * HEAD_DIM ** (-0.5)
    allowed = segment_ids[:, :, None] == segment_ids[:, None, :]
    scores = jnp.where(allowed[:, None], scores, -1e+30)
    top_score = lax.stop_gradient(lax.optimization_barrier(jnp.max(scores, axis=-1, keepdims=True)))
    exponent = jnp.exp(scores - top_score)
    probable = (exponent / lax.optimization_barrier(jnp.sum(exponent, axis=-1, keepdims=True))).astype(jnp.bfloat16)
    mixed_heads = jnp.einsum('bhqk,bkhd->bqhd', probable.astype(jnp.float32), values_all)
    return mixed_heads.reshape(pack_count, pack_length, model_width).astype(jnp.bfloat16)

def contract_rows(left_side, right_side):
    return lax.dot_general(left_side, right_side, (((0,), (0,)), ((), ())), preferred_element_type=jnp.float32)

def contract_cols(left_side, right_side):
    return lax.dot_general(left_side, right_side, (((1,), (1,)), ((), ())), preferred_element_type=jnp.float32)

def layer_backward(patches, cotangent, segment_ids, norm_gain, qkv_weight, out_weight):
    pack_count, pack_length, model_width = patches.shape
    inputs = patches.astype(jnp.float32)
    normed, norm_pullback = jax.vjp(normalize, inputs, norm_gain)
    flat_hidden = normed.astype(jnp.bfloat16).reshape(-1, model_width)
    projected = jnp.dot(flat_hidden, qkv_weight, preferred_element_type=jnp.float32).astype(jnp.bfloat16)
    projected = projected.reshape(pack_count, pack_length, 3 * model_width)

    def attend_pack(stacked):
        return attend(stacked, segment_ids)
    attended, attend_pullback = jax.vjp(attend_pack, projected)
    flat_cotangent = cotangent.reshape(-1, model_width)
    grad_attended = contract_cols(flat_cotangent, out_weight).astype(jnp.bfloat16)
    grad_projected = attend_pullback(grad_attended.reshape(attended.shape))[0]
    flat_grad = grad_projected.reshape(-1, 3 * model_width)
    grad_hidden = contract_cols(flat_grad, qkv_weight)
    gain_term = norm_pullback(grad_hidden.reshape(normed.shape))[1]
    return (flat_hidden, flat_grad, attended.reshape(-1, model_width), gain_term)

def sign_values(sign_bits):
    return (1 - 2 * sign_bits).astype(jnp.float32)

def rotate(matrix, sign_bits):
    signed = matrix * sign_values(sign_bits)
    blocks = signed.reshape(-1, BLOCK_WIDTH)
    return jnp.dot(blocks, hadamard_table(), precision=lax.Precision.HIGHEST).reshape(matrix.shape)

def clip_blocks(rotated):
    blocks = rotated.reshape(-1, BLOCK_WIDTH)
    clip_bound = CLIP_RATIO * jnp.sqrt(lax.optimization_barrier(jnp.mean(blocks * blocks, axis=-1, keepdims=True)) + EPSILON)
    return jnp.clip(blocks, -clip_bound, clip_bound).reshape(rotated.shape)

def decode(summed, sign_bits):
    blocks = summed.reshape(-1, BLOCK_WIDTH)
    turned = jnp.dot(blocks, hadamard_table(), precision=lax.Precision.HIGHEST).reshape(summed.shape)
    return turned * sign_values(sign_bits)

def reference(patches, cotangent, segment_ids, live_packs, norm_gain, qkv_weight, out_weight, signs_qkv, signs_out):
    model_width = patches.shape[-1]

    def by_device(array):
        return array.reshape((N_OUTER, N_INNER, PACKS_DEV) + array.shape[1:])
    live_grid = live_packs.reshape(N_OUTER, N_INNER)

    def device_step(running, inputs):
        sum_qkv, sum_out, sum_gain = running
        pack_inputs, pack_cotangent, pack_segments, live_count = inputs
        live_mask = (jnp.arange(PACKS_DEV, dtype=jnp.int32) < live_count).astype(jnp.bfloat16)
        masked = pack_cotangent * live_mask[:, None, None]
        hidden, grad_projected, attended, gain_term = layer_backward(pack_inputs, masked, pack_segments, norm_gain, qkv_weight, out_weight)
        term_qkv = contract_rows(hidden, grad_projected)
        term_out = contract_rows(attended, masked.reshape(-1, model_width))
        term_qkv = lax.optimization_barrier(term_qkv.astype(jnp.bfloat16)).astype(jnp.float32)
        term_out = lax.optimization_barrier(term_out.astype(jnp.bfloat16)).astype(jnp.float32)
        return ((sum_qkv + term_qkv, sum_out + term_out, sum_gain + gain_term), None)

    def group_step(running, inputs):
        total_qkv, total_out, total_gain = running
        initial = (jnp.zeros((model_width, 3 * model_width), jnp.float32), jnp.zeros((model_width, model_width), jnp.float32), jnp.zeros((model_width,), jnp.float32))
        group_qkv, group_out, group_gain = lax.scan(device_step, initial, inputs)[0]
        total_qkv = total_qkv + clip_blocks(rotate(group_qkv, signs_qkv))
        total_out = total_out + clip_blocks(rotate(group_out, signs_out))
        return ((total_qkv, total_out, total_gain + group_gain), None)
    initial = (jnp.zeros((model_width, 3 * model_width), jnp.float32), jnp.zeros((model_width, model_width), jnp.float32), jnp.zeros((model_width,), jnp.float32))
    inputs = (by_device(patches), by_device(cotangent), by_device(segment_ids), live_grid)
    total_qkv, total_out, total_gain = lax.scan(group_step, initial, inputs)[0]
    return (decode(total_qkv, signs_qkv), decode(total_out, signs_out), total_gain)
```

```python
import functools

import jax
import jax.numpy as jnp
from jax import lax
from jax.experimental import pallas as pl
from jax.experimental.pallas import tpu as pltpu
from jax.sharding import Mesh
from jax.sharding import PartitionSpec as P

INNER = ("inner_0", "inner_1")
OUTER = ("outer_0", "outer_1")
OUTER_INNER = ("outer_0", "outer_1", "inner_0", "inner_1")


D = 1024
L = 128
SLOTS = 4
ROWS = SLOTS * L
EPSILON = 1e-06
CLIP_RATIO = 2.0
BLOCK = 128
BLOCK_SCALE = 0.08838834764831845
MASKED = -1e30
PAIRS_A = 5
PAIRS_B = 3
COLS_A = PAIRS_A * 128
COLS_B = PAIRS_B * 128
WIDTH_A = 3 * COLS_A
WIDTH_B = 3 * COLS_B + D

F32 = jnp.float32
BF16 = jnp.bfloat16
VMEM = pl.BlockSpec(memory_space=pltpu.VMEM)
SMEM = pl.BlockSpec(memory_space=pltpu.SMEM)
HBM = pl.BlockSpec(memory_space=pl.ANY)
PARAMS = pltpu.CompilerParams(vmem_limit_bytes=56 * 1024 * 1024)


def mm(a, b, ca=1, cb=0):
    return lax.dot_general(a, b, (((ca,), (cb,)), ((), ())), preferred_element_type=F32)


def prep_kernel(live_ref, x_ref, cot_ref, seg_ref, gain_ref, h_ref, ht_ref, cm_ref, bias_ref):
    gain = gain_ref[...]
    for p in range(SLOTS):
        rows = pl.ds(p * L, L)
        x = x_ref[rows, :].astype(F32)
        center = x - jnp.mean(x, axis=-1, keepdims=True)
        spread = jnp.mean(center * center, axis=-1, keepdims=True)
        h = (center * lax.rsqrt(spread + EPSILON) * gain).astype(BF16)
        h_ref[rows, :] = h
        ht_ref[:, rows] = h.T
        live = (live_ref[0] > p).astype(F32)
        cm_ref[rows, :] = (cot_ref[rows, :].astype(F32) * live).astype(BF16)
        across = jnp.broadcast_to(seg_ref[p : p + 1, :].astype(F32), (L, L))
        bias_ref[rows, :] = jnp.where(across == across.T, 0.0, MASKED)


def prep(live, patches, cotangent, segments, gain):
    return pl.pallas_call(
        prep_kernel,
        out_shape=(
            jax.ShapeDtypeStruct((ROWS, D), BF16),
            jax.ShapeDtypeStruct((D, ROWS), BF16),
            jax.ShapeDtypeStruct((ROWS, D), BF16),
            jax.ShapeDtypeStruct((ROWS, L), F32),
        ),
        in_specs=[SMEM, VMEM, VMEM, VMEM, VMEM],
        out_specs=(VMEM,) * 4,
        compiler_params=PARAMS,
        name="prep",
    )(live, patches, cotangent, segments, gain)


def fetch(ids_ref, pieces, x_first, first_col, width, dst, sem):
    a, b = (ids_ref[0], ids_ref[1]) if x_first else (ids_ref[1], ids_ref[0])
    core = ids_ref[2]
    copies = []
    for side in range(2):
        half = core if side == 0 else 1 - core
        for k in range(4):
            src = pieces[side * 4 + k]
            second = lax.rem(b + 4 - k, 4)
            for j in range(4):
                first = lax.rem(a + 4 - j, 4)
                shard = first * 4 + second if x_first else second * 4 + first
                row = pl.multiple_of(shard * 64 + half * 32, 32)
                copies.append(
                    pltpu.make_async_copy(
                        src.at[j, :, pl.ds(first_col, width)], dst.at[pl.ds(row, 32), :], sem
                    )
                )
    for c in copies:
        c.start()
    return copies


def attend_pairs(pairs, q_ref, k_ref, v_ref, kt_ref, vt_ref, do_ref, bias_ref, dqt_ref, dk_ref, dv_ref, ot_ref, ot_row):
    low = lax.broadcasted_iota(jnp.int32, (L, 128), 1) < 64
    top = lax.broadcasted_iota(jnp.int32, (128, L), 0) < 64
    zero = jnp.zeros((L, 128), BF16)

    def visit(p, carry):
        rows = pl.ds(pl.multiple_of(p * L, L), L)
        bias = bias_ref[rows, :]
        for i in range(pairs):
            cols = slice(i * 128, (i + 1) * 128)
            q, k, v = q_ref[rows, cols], k_ref[rows, cols], v_ref[rows, cols]
            do = do_ref[rows, cols]
            kt, vt = kt_ref[cols, rows], vt_ref[cols, rows]
            k2 = jnp.concatenate([jnp.where(low, k, zero), jnp.where(low, zero, k)], axis=0)
            v2 = jnp.concatenate([jnp.where(low, v, zero), jnp.where(low, zero, v)], axis=0)
            kt2 = jnp.concatenate([jnp.where(top, kt, zero), jnp.where(top, zero, kt)], axis=1)
            vt2 = jnp.concatenate([jnp.where(top, vt, zero), jnp.where(top, zero, vt)], axis=1)
            scores = mm(k2, q, 1, 1)
            dprob = mm(v2, do, 1, 1)
            probs, dscores = [], []
            for h in range(2):
                s = scores[h * 128 : (h + 1) * 128, :] + bias
                e = jnp.exp(s - jnp.max(s, axis=0, keepdims=True))
                prob = e * (1.0 / jnp.sum(e, axis=0, keepdims=True))
                dp = dprob[h * 128 : (h + 1) * 128, :]
                ds = prob * (dp - jnp.sum(prob * dp, axis=0, keepdims=True))
                probs.append(prob.astype(BF16))
                dscores.append(ds.astype(BF16))
            prob = jnp.concatenate(probs, axis=0)
            ds = jnp.concatenate(dscores, axis=0)
            ot_ref[pl.ds(ot_row + i * 128, 128), rows] = mm(vt2, prob).astype(BF16)
            dqt_ref[cols, rows] = (mm(kt2, ds) * 0.125).astype(BF16)
            dv = mm(prob, do)
            dk = mm(ds, q)
            dv_ref[rows, cols] = jnp.where(low, dv[:128], dv[128:]).astype(BF16)
            dk_ref[rows, cols] = jnp.where(low, dk[:128], dk[128:]).astype(BF16)
        return carry

    lax.fori_loop(0, SLOTS, visit, 0)


def project(h_ref, w_ref, cols, q_ref, k_ref, v_ref, kt_ref, vt_ref):
    h = h_ref[...]
    q_ref[...] = (mm(h, w_ref[:, 0:cols]).astype(BF16).astype(F32) * 0.125).astype(BF16)
    k_ref[...] = mm(h, w_ref[:, cols : 2 * cols]).astype(BF16)
    kt_ref[...] = k_ref[...].T
    v_ref[...] = mm(h, w_ref[:, 2 * cols : 3 * cols]).astype(BF16)
    vt_ref[...] = v_ref[...].T


def gain_terms(g, w):
    total = None
    for c in range(0, g.shape[1], 128):
        term = g[:, c : c + 128] * w[:, c : c + 128].astype(F32)
        total = term if total is None else total + term
    return total


def scratch_of(cols):
    return [pltpu.VMEM((ROWS, cols), BF16)] * 3 + [pltpu.VMEM((cols, ROWS), BF16)] * 2 + [
        pltpu.VMEM((cols, ROWS), BF16),
        pltpu.VMEM((ROWS, cols), BF16),
        pltpu.VMEM((ROWS, cols), BF16),
    ]


def first_kernel(ids_ref, h_ref, ht_ref, cm_ref, bias_ref, *rest):
    pieces_a, pieces_b = rest[:8], rest[8:16]
    outs, ot_ref, do_b_ref, gacc_ref = rest[16:20], rest[20], rest[21], rest[22]
    w_ref, wo_ref, do_ref, sem_a, sem_b = rest[23:28]
    q_ref, k_ref, v_ref, kt_ref, vt_ref, dqt_ref, dk_ref, dv_ref = rest[28:]
    copies_a = fetch(ids_ref, pieces_a, True, 0, WIDTH_A, w_ref, sem_a)
    copies_b = fetch(ids_ref, pieces_b, False, 3 * COLS_B, D, wo_ref, sem_b)
    for c in copies_a:
        c.wait()
    project(h_ref, w_ref, COLS_A, q_ref, k_ref, v_ref, kt_ref, vt_ref)
    for c in copies_b:
        c.wait()
    cm = cm_ref[...]
    do_ref[...] = mm(cm, wo_ref[:COLS_A, :], 1, 1).astype(BF16)
    do_b_ref[...] = mm(cm, wo_ref[COLS_A:, :], 1, 1).astype(BF16)
    attend_pairs(PAIRS_A, q_ref, k_ref, v_ref, kt_ref, vt_ref, do_ref, bias_ref, dqt_ref, dk_ref, dv_ref, ot_ref, 0)
    x = ids_ref[0]
    for j in range(4):
        block = pl.ds(pl.multiple_of(lax.rem(x + j, 4) * 256, 256), 256)
        lhs = ht_ref[block, :]
        total = None
        for n, (rhs, cb) in enumerate(((dqt_ref, 1), (dk_ref, 0), (dv_ref, 0))):
            g = mm(lhs, rhs[...], 1, cb)
            outs[j][:, n * COLS_A : (n + 1) * COLS_A] = g.astype(BF16)
            term = gain_terms(g, w_ref[block, n * COLS_A : (n + 1) * COLS_A])
            total = term if total is None else total + term
        gacc_ref[block, :] = total


def first_part(ids, h, ht, cm, bias, pieces_a, pieces_b):
    return pl.pallas_call(
        first_kernel,
        out_shape=tuple(jax.ShapeDtypeStruct((256, WIDTH_A), BF16) for _ in range(4))
        + (
            jax.ShapeDtypeStruct((COLS_A, ROWS), BF16),
            jax.ShapeDtypeStruct((ROWS, COLS_B), BF16),
            jax.ShapeDtypeStruct((D, 128), F32),
        ),
        in_specs=[SMEM] + [VMEM] * 4 + [HBM] * 16,
        out_specs=(VMEM,) * 7,
        scratch_shapes=[
            pltpu.VMEM((D, WIDTH_A), BF16),
            pltpu.VMEM((D, D), BF16),
            pltpu.VMEM((ROWS, COLS_A), BF16),
            pltpu.SemaphoreType.DMA,
            pltpu.SemaphoreType.DMA,
        ]
        + scratch_of(COLS_A),
        compiler_params=PARAMS,
        name="first_part",
    )(ids, h, ht, cm, bias, *pieces_a, *pieces_b)


def second_kernel(ids_ref, h_ref, ht_ref, cm_ref, bias_ref, ot_a_ref, do_ref, *rest):
    pieces_b = rest[:8]
    outs, gacc_ref = rest[8:12], rest[12]
    w_ref, ot_ref, sem_b = rest[13:16]
    q_ref, k_ref, v_ref, kt_ref, vt_ref, dqt_ref, dk_ref, dv_ref = rest[16:]
    copies_b = fetch(ids_ref, pieces_b, False, 0, 3 * COLS_B, w_ref, sem_b)
    ot_ref[:COLS_A, :] = ot_a_ref[...]
    for c in copies_b:
        c.wait()
    project(h_ref, w_ref, COLS_B, q_ref, k_ref, v_ref, kt_ref, vt_ref)
    attend_pairs(
        PAIRS_B, q_ref, k_ref, v_ref, kt_ref, vt_ref, do_ref, bias_ref, dqt_ref, dk_ref, dv_ref, ot_ref, COLS_A
    )
    y = ids_ref[1]
    for j in range(4):
        blocks = [pl.ds(pl.multiple_of(x * 256 + lax.rem(y + j, 4) * 64, 64), 64) for x in range(4)]
        lhs = jnp.concatenate([ht_ref[b, :] for b in blocks], axis=0)
        lhs_out = jnp.concatenate([ot_ref[b, :] for b in blocks], axis=0)
        total = None
        for n, (rhs, cb) in enumerate(((dqt_ref, 1), (dk_ref, 0), (dv_ref, 0))):
            g = mm(lhs, rhs[...], 1, cb)
            outs[j][:, n * COLS_B : (n + 1) * COLS_B] = g.astype(BF16)
            w = jnp.concatenate([w_ref[b, n * COLS_B : (n + 1) * COLS_B] for b in blocks], axis=0)
            term = gain_terms(g, w)
            total = term if total is None else total + term
        for x in range(4):
            gacc_ref[blocks[x], :] = total[x * 64 : (x + 1) * 64, :]
        outs[j][:, 3 * COLS_B :] = mm(lhs_out, cm_ref[...]).astype(BF16)


def second_part(ids, h, ht, cm, bias, ot_a, do_b, pieces_b):
    return pl.pallas_call(
        second_kernel,
        out_shape=tuple(jax.ShapeDtypeStruct((256, WIDTH_B), BF16) for _ in range(4))
        + (jax.ShapeDtypeStruct((D, 128), F32),),
        in_specs=[SMEM] + [VMEM] * 6 + [HBM] * 8,
        out_specs=(VMEM,) * 5,
        scratch_shapes=[
            pltpu.VMEM((D, 3 * COLS_B), BF16),
            pltpu.VMEM((D, ROWS), BF16),
            pltpu.SemaphoreType.DMA,
        ]
        + scratch_of(COLS_B),
        compiler_params=PARAMS,
        name="second_part",
    )(ids, h, ht, cm, bias, ot_a, do_b, *pieces_b)


def fold_kernel(at_ref, *refs):
    arrived, outs, scratch = refs[:4], refs[4:8], refs[8]
    total = arrived[0][...].astype(F32)
    for r in arrived[1:]:
        total = total + r[...].astype(F32)
    scratch[...] = total.astype(BF16)
    for j in range(4):
        outs[j][...] = scratch[pl.ds(pl.multiple_of(lax.rem(at_ref[0] + j, 4) * 64, 64), 64), :]


def fold(at, arrived):
    width = arrived[0].shape[1]
    return pl.pallas_call(
        fold_kernel,
        out_shape=tuple(jax.ShapeDtypeStruct((64, width), BF16) for _ in range(4)),
        in_specs=[SMEM] + [VMEM] * 4,
        out_specs=(VMEM,) * 4,
        scratch_shapes=[pltpu.VMEM((256, width), BF16)],
        compiler_params=PARAMS,
        name="fold",
    )(at, *arrived)


def hadamard():
    a = lax.broadcasted_iota(jnp.int32, (BLOCK, BLOCK), 0)
    b = lax.broadcasted_iota(jnp.int32, (BLOCK, BLOCK), 1)
    common = a & b
    odd = jnp.zeros_like(common)
    for level in range(7):
        odd = odd ^ ((common >> level) & 1)
    return (1 - 2 * odd).astype(F32).astype(BF16)


def turn(v, table):
    high = v.astype(BF16)
    low = (v - high.astype(F32)).astype(BF16)
    return (mm(high, table) + mm(low, table)) * BLOCK_SCALE


def clip_kernel(ids_ref, sign_ref, *refs):
    first, second, keep_ref, send_ref, scratch = refs[:4], refs[4:8], refs[8], refs[9], refs[10]
    table = hadamard()
    for arrived, width, at in ((first, WIDTH_A, 0), (second, WIDTH_B, WIDTH_A)):
        for c in range(0, width, BLOCK):
            total = arrived[0][:, c : c + BLOCK].astype(F32)
            for r in arrived[1:]:
                total = total + r[:, c : c + BLOCK].astype(F32)
            turned = turn(total * sign_ref[:, at + c : at + c + BLOCK], table)
            bound = CLIP_RATIO * jnp.sqrt(jnp.mean(turned * turned, axis=-1, keepdims=True) + EPSILON)
            scratch[:, at + c : at + c + BLOCK] = jnp.clip(turned, -bound, bound).astype(BF16)
    core = ids_ref[2]
    keep_ref[...] = scratch[pl.ds(pl.multiple_of(core * 32, 32), 32), :]
    send_ref[...] = scratch[pl.ds(pl.multiple_of((1 - core) * 32, 32), 32), :]


def clip_rotated(ids, signs, first, second):
    return pl.pallas_call(
        clip_kernel,
        out_shape=(jax.ShapeDtypeStruct((32, 4 * D), BF16),) * 2,
        in_specs=[SMEM] + [VMEM] * 9,
        out_specs=(VMEM,) * 2,
        scratch_shapes=[pltpu.VMEM((64, 4 * D), BF16)],
        compiler_params=PARAMS,
        name="clip_rotated",
    )(ids, signs, *first, *second)


def decode_kernel(sign_ref, *refs):
    arrived, out_ref = refs[:4], refs[4]
    table = hadamard()
    for c in range(0, 4 * D, BLOCK):
        total = arrived[0][:, c : c + BLOCK].astype(F32)
        for r in arrived[1:]:
            total = total + r[:, c : c + BLOCK].astype(F32)
        out_ref[:, c : c + BLOCK] = (turn(total, table) * sign_ref[:, c : c + BLOCK]).astype(BF16)


def decode(signs, arrived):
    return pl.pallas_call(
        decode_kernel,
        out_shape=jax.ShapeDtypeStruct((32, 4 * D), BF16),
        in_specs=[VMEM] * 5,
        out_specs=VMEM,
        compiler_params=PARAMS,
        name="decode",
    )(signs, *arrived)


def place_kernel(ids_ref, own_ref, other_ref, qkv_ref, out_ref):
    core = ids_ref[2]
    for ref, half in ((own_ref, core), (other_ref, 1 - core)):
        rows = pl.ds(pl.multiple_of(half * 32, 32), 32)
        for n in range(3):
            qkv_ref[rows, n * D : n * D + COLS_A] = ref[:, n * COLS_A : (n + 1) * COLS_A].astype(F32)
            qkv_ref[rows, n * D + COLS_A : (n + 1) * D] = ref[
                :, WIDTH_A + n * COLS_B : WIDTH_A + (n + 1) * COLS_B
            ].astype(F32)
        out_ref[rows, :] = ref[:, WIDTH_A + 3 * COLS_B :].astype(F32)


def place(ids, own, other):
    return pl.pallas_call(
        place_kernel,
        out_shape=(jax.ShapeDtypeStruct((64, 3 * D), F32), jax.ShapeDtypeStruct((64, D), F32)),
        in_specs=[SMEM, VMEM, VMEM],
        out_specs=(VMEM,) * 2,
        compiler_params=PARAMS,
        name="place",
    )(ids, own, other)


def shift(value, axis, by):
    size = lax.axis_size(axis)
    return lax.ppermute(value, axis, [(i, (i + by) % size) for i in range(size)])


def swap(value):
    return shift(value, "outer_1", 1)


def gather_shard(own, first_axis, second_axis):
    stack = jnp.stack([own] + [shift(own, first_axis, by) for by in (1, 2, 3)])
    mine = [stack] + [shift(stack, second_axis, by) for by in (1, 2, 3)]
    return mine + [swap(m) for m in mine]


def scatter_phase(pieces, axis):
    return [pieces[0]] + [shift(pieces[by], axis, by) for by in (1, 2, 3)]


def columns_of(qkv, out):
    thirds = [qkv[:, n * D : (n + 1) * D] for n in range(3)]
    first = jnp.concatenate([t[:, :COLS_A] for t in thirds], axis=1)
    second = jnp.concatenate([t[:, COLS_A:] for t in thirds] + [out], axis=1)
    return first, second


def on_device(patches, cotangent, segment_ids, live_packs, norm_gain, qkv_weight, out_weight, signs_qkv, signs_out):
    x, y, core = (lax.axis_index(a) for a in ("inner_0", "inner_1", "outer_1"))
    ids = jnp.stack([x, y, core]).astype(jnp.int32)
    half_a, half_b = columns_of(
        lax.dynamic_slice_in_dim(qkv_weight, core * 32, 32, 0), lax.dynamic_slice_in_dim(out_weight, core * 32, 32, 0)
    )
    pieces_a = gather_shard(half_a, "inner_0", "inner_1")
    pieces_b = gather_shard(half_b, "inner_1", "inner_0")
    h, ht, cm, bias = prep(
        live_packs, patches.reshape(ROWS, D), cotangent.reshape(ROWS, D), segment_ids, norm_gain.reshape(1, D)
    )
    *grads_a, ot_a, do_b, gacc_a = first_part(ids, h, ht, cm, bias, pieces_a, pieces_b)
    *grads_b, gacc_b = second_part(ids, h, ht, cm, bias, ot_a, do_b, pieces_b)
    gain_grad = jnp.sum(gacc_a + gacc_b, axis=1) / norm_gain
    for axis in OUTER_INNER:
        gain_grad = lax.psum(gain_grad, axis)
    folded_a = fold(y.reshape(1), scatter_phase(grads_a, "inner_0"))
    folded_b = fold(x.reshape(1), scatter_phase(grads_b, "inner_1"))
    sums_a = scatter_phase(folded_a, "inner_1")
    sums_b = scatter_phase(folded_b, "inner_0")
    signs = jnp.concatenate(columns_of(signs_qkv.reshape(1, -1), signs_out.reshape(1, -1)), axis=1)
    signs = (1 - 2 * signs).astype(F32)
    keep, send = clip_rotated(ids, signs, sums_a, sums_b)
    paired = (keep.astype(F32) + swap(send).astype(F32)).astype(BF16)
    own = decode(signs, [paired] + [shift(paired, "outer_0", by) for by in (1, 2, 3)])
    qkv_grad, out_grad = place(ids, own, swap(own))
    return qkv_grad, out_grad, gain_grad


def solution(mesh):
    finer = Mesh(mesh.devices.reshape(4, 2, 4, 4), OUTER_INNER)
    placed = (
        P(OUTER_INNER, None, None),
        P(OUTER_INNER, None, None),
        P(OUTER_INNER, None),
        P(OUTER_INNER),
        P(),
        P(INNER, None),
        P(INNER, None),
        P(),
        P(),
    )
    return jax.shard_map(
        on_device,
        mesh=finer,
        in_specs=placed,
        out_specs=(P(INNER, None), P(INNER, None), P()),
        check_vma=False,
    )
```
